512 devices in a mesh: tm: 64 (over z, x), head: 8 (over y, core).
Axes of the slice: x: 4, y: 4, z: 16, core: 2. Of those that a mesh axis runs over, the one named last changes fastest.
Arguments:
- frames: bfloat16 [131072, 1024], P('tm'), may hold values from -6 to 6
- conv_weight: bfloat16 [4, 1024], replicated, may hold values from -3 to 3
- w_query: bfloat16 [1024, 1024], P(None, 'head'), may hold values from -0.1875 to 0.1875
- w_key: bfloat16 [1024, 1024], P(None, 'head'), may hold values from -0.1875 to 0.1875
- w_value: bfloat16 [1024, 1024], P(None, 'head'), may hold values from -0.1875 to 0.1875
- w_gate: bfloat16 [1024, 1024], P(None, 'head'), may hold values from -0.1875 to 0.1875
- w_out: bfloat16 [1024, 1024], P('head'), may hold values from -0.1875 to 0.1875
- norm_gain: float32 [1024], P('head'), may hold values from 0.1 to 1.9
Outputs:
- layer_out: bfloat16 [131072, 1024], P('tm', 'head')
The draws below stay inside these ranges and needn't reach their ends.
All inputs are finite; a program needn't handle non-finite values.
Results may differ from the reference program's by a relative error of at most 0.014.
Values may be sent and summed in bfloat16 or wider, within the bound.
No kernel may reach another device: no remote copies, remote signals or barrier semaphores. Data moves between devices by JAX's collectives and lax.ppermute only.
A program may use at most 64 MiB of HBM per device.

```python
import jax
import jax.numpy as jnp
from jax import lax

D = 1024
HEADS = 8
HEAD_DIM = 128
CONV = 4
BLOCK = 512
SEQ = 131072
N_HEAD = 8


def block_scale(rng, shape, shards, low, top_value):
    def one(position, shards_of):
        heights = jax.random.uniform(jax.random.fold_in(jax.random.fold_in(rng, 6), position), (shards_of,), jnp.float32, low / len(shards), top_value / len(shards))
        return jnp.repeat(jnp.exp(heights), shape[position] // shards_of).reshape((-1,) + (1,) * (len(shape) - position - 1))

    loudness = one(*shards[0])
    for cut in shards[1:]:
        loudness = loudness * one(*cut)
    return loudness


def centred(stream_key, shape, scale, bound, shards=(), held_as=jnp.bfloat16):
    values = scale * jax.random.normal(stream_key, shape, jnp.float32)
    if shards:
        values = values * block_scale(stream_key, shape, shards, -0.22, 0.18)
    return jnp.clip(values, -bound, bound).astype(held_as)


def setup_inputs(seed: int = 0) -> dict:
    streams_of = jax.random.split(jax.random.key(seed), 9)
    return {
        "frames": centred(streams_of[0], (SEQ, D), 1.0, 6.0, ((0, 64),)),
        "conv_weight": centred(streams_of[1], (CONV, D), 0.5, 3.0),
        "w_query": centred(streams_of[2], (D, D), D ** -0.5, 0.1875, ((1, 8),)),
        "w_key": centred(streams_of[3], (D, D), D ** -0.5, 0.1875, ((1, 8),)),
        "w_value": centred(streams_of[4], (D, D), D ** -0.5, 0.1875, ((1, 8),)),
        "w_gate": centred(streams_of[5], (D, D), D ** -0.5, 0.1875, ((1, 8),)),
        "w_out": centred(streams_of[6], (D, D), D ** -0.5, 0.1875, ((0, 8),)),
        "norm_gain": jnp.clip(1.0 + 0.18 * jax.random.normal(streams_of[7], (D,), jnp.float32), 0.1, 1.9),
    }


def feature_map(inputs):
    return jnp.where(inputs > 0, inputs + 1.0, jnp.exp(jnp.minimum(inputs, 0.0)))

def reference(frames, conv_weight, w_query, w_key, w_value, w_gate, w_out, norm_gain):
    padded = jnp.concatenate([jnp.zeros((CONV - 1, D), jnp.float32), frames.astype(jnp.float32)], axis=0)
    taps = conv_weight.astype(jnp.float32)
    mixed = taps[0] * padded[0:SEQ]
    for offset in range(1, CONV):
        mixed = mixed + taps[offset] * padded[offset:offset + SEQ]
    smooth = mixed.astype(jnp.bfloat16)
    queries = feature_map(jnp.dot(smooth, w_query, preferred_element_type=jnp.float32)).astype(jnp.bfloat16)
    key_feats = feature_map(jnp.dot(smooth, w_key, preferred_element_type=jnp.float32)).astype(jnp.bfloat16)
    values = jnp.dot(smooth, w_value, preferred_element_type=jnp.float32).astype(jnp.bfloat16)
    gates = jnp.dot(smooth, w_gate, preferred_element_type=jnp.float32)
    blocks = SEQ // BLOCK
    block_shape = (blocks, BLOCK, HEADS, HEAD_DIM)
    causal = jnp.tril(jnp.ones((BLOCK, BLOCK), jnp.bool_))

    def advance(kv_state, inputs):
        query_blk = inputs[0].astype(jnp.float32)
        key_blk = inputs[1].astype(jnp.float32)
        value_blk = inputs[2].astype(jnp.float32)
        scores = jnp.einsum('thd,shd->hts', query_blk, key_blk)
        scores = jnp.where(causal[None], scores, 0.0).astype(jnp.bfloat16).astype(jnp.float32)
        carried = kv_state.astype(jnp.bfloat16).astype(jnp.float32)
        result = jnp.einsum('hts,shd->thd', scores, value_blk) + jnp.einsum('thd,hde->the', query_blk, carried)
        kv_state = kv_state + jnp.einsum('thd,the->hde', key_blk, value_blk)
        return (kv_state, result)
    start_state = jnp.zeros((HEADS, HEAD_DIM, HEAD_DIM), jnp.float32)
    _, outputs = lax.scan(advance, start_state, (queries.reshape(block_shape), key_feats.reshape(block_shape), values.reshape(block_shape)))
    attended = outputs.reshape(SEQ, HEADS, HEAD_DIM)
    mean_square = lax.optimization_barrier(jnp.mean(attended * attended, axis=-1, keepdims=True))
    normed = attended * lax.rsqrt(mean_square + 1e-06) * norm_gain.reshape(HEADS, HEAD_DIM)
    normed = normed * jax.nn.silu(gates).reshape(SEQ, HEADS, HEAD_DIM)
    gated = normed.reshape(SEQ, D).astype(jnp.bfloat16)
    width = D // N_HEAD
    total = jnp.zeros((SEQ, D), jnp.float32)
    for group_index in range(N_HEAD):
        lower = group_index * width
        partial_value = jnp.dot(gated[:, lower:lower + width], w_out[lower:lower + width], preferred_element_type=jnp.float32)
        total = total + partial_value.astype(jnp.bfloat16).astype(jnp.float32)
    return total.astype(jnp.bfloat16)
```

```python
import functools

import jax
import jax.numpy as jnp
from jax import lax
from jax.experimental import pallas as pl
from jax.experimental.pallas import tpu as pltpu
from jax.sharding import PartitionSpec as P

HEAD_DIM = 128
CONV = 4
BLOCK = 512
CORES = 2
EDGE = 16
LANES = 128
TILE = 256
PER_BLOCK = BLOCK // TILE
MOST_VMEM = 44 << 20

F32 = jnp.float32
BF16 = jnp.bfloat16


def feature_map(inputs):
    return jnp.where(inputs > 0, inputs + 1.0, jnp.exp(jnp.minimum(inputs, 0.0)))


def join_weights(refs, joined):
    for place, ref in enumerate(refs):
        joined[:, place * HEAD_DIM : (place + 1) * HEAD_DIM] = ref[...]


def projections(frames_ref, edge, taps_ref, joined, smooth, outs):
    width = frames_ref.shape[1]
    for lane in range(0, width, LANES):
        cols = slice(lane, lane + LANES)
        own = frames_ref[:, cols].astype(F32)
        padded = jnp.concatenate([edge[EDGE - 8 :, cols], own], axis=0)
        taps = taps_ref[:, cols].astype(F32)
        mixed = taps[0:1] * padded
        for offset in range(1, CONV):
            mixed = pltpu.roll(mixed, 1, 0) + taps[offset : offset + 1] * padded
        smooth[:, cols] = mixed[8:].astype(BF16)
    product = jnp.dot(smooth[...], joined[...], preferred_element_type=F32)
    q_ref, k_ref, v_ref, g_ref = outs
    keys = feature_map(product[:, 0:HEAD_DIM]).astype(BF16)
    values = product[:, HEAD_DIM : 2 * HEAD_DIM].astype(BF16)
    q_ref[...] = feature_map(product[:, 2 * HEAD_DIM : 3 * HEAD_DIM]).astype(BF16)
    k_ref[...] = keys
    v_ref[...] = values
    g_ref[...] = product[:, 3 * HEAD_DIM :]
    return lax.dot_general(
        keys, values, (((0,), (0,)), ((), ())), preferred_element_type=F32
    )


def later_kernel(
    frames_ref, before_ref, taps_ref, wk, wv, wq, wg, q_ref, k_ref, v_ref, g_ref, state_ref,
    joined, smooth,
):
    step = pl.program_id(0)

    @pl.when(step == 0)
    def _():
        join_weights((wk, wv, wq, wg), joined)

    edge = before_ref[...].astype(F32)
    state = projections(
        frames_ref, edge, taps_ref, joined, smooth, (q_ref, k_ref, v_ref, g_ref)
    )

    @pl.when(step % PER_BLOCK == 0)
    def _():
        state_ref[0] = state

    @pl.when(step % PER_BLOCK != 0)
    def _():
        state_ref[0] += state


def first_kernel(
    frames_ref, before_ref, edge_ref, taps_ref, wk, wv, wq, wg, states_ref, q_in, k_in, v_in, g_in,
    q_ref, k_ref, v_ref, g_ref, state_ref, total_ref, joined, smooth,
):
    step = pl.program_id(0)

    @pl.when(step == 0)
    def _():
        join_weights((wk, wv, wq, wg), joined)

    edge = jnp.where(step == 0, edge_ref[...].astype(F32), before_ref[...].astype(F32))
    state = projections(
        frames_ref, edge, taps_ref, joined, smooth, (q_ref, k_ref, v_ref, g_ref)
    )

    @pl.when(step == 0)
    def _():
        state_ref[...] = state
        total_ref[...] = state + jnp.sum(states_ref[...], axis=0)

    @pl.when(step != 0)
    def _():
        state_ref[...] += state
        total_ref[...] += state


def front(frames, edge, taps, weights):
    rows, width = frames.shape
    blocks = rows // BLOCK
    per = TILE // EDGE
    whole = lambda a: pl.BlockSpec(a.shape, lambda i: (0,) * a.ndim)
    tile = lambda n: pl.BlockSpec((TILE, n), lambda i: (i + PER_BLOCK, 0))
    square = jax.ShapeDtypeStruct((HEAD_DIM, HEAD_DIM), F32)
    long_shapes = [pltpu.HBM((rows, HEAD_DIM), BF16)] * 3 + [pltpu.HBM((rows, HEAD_DIM), F32)]
    scratch = [pltpu.VMEM((width, 4 * HEAD_DIM), BF16), pltpu.VMEM((TILE, width), BF16)]
    flops = 2 * BLOCK * width * 4 * HEAD_DIM
    *longs, states = pl.pallas_call(
        later_kernel,
        grid=((blocks - 1) * PER_BLOCK,),
        in_specs=[
            tile(width),
            pl.BlockSpec((EDGE, width), lambda i: ((i + PER_BLOCK) * per - 1, 0)),
            whole(taps),
        ]
        + [whole(w) for w in weights],
        out_specs=[tile(HEAD_DIM)] * 4
        + [pl.BlockSpec((1, HEAD_DIM, HEAD_DIM), lambda i: (i // PER_BLOCK, 0, 0))],
        out_shape=long_shapes + [jax.ShapeDtypeStruct((blocks - 1, HEAD_DIM, HEAD_DIM), F32)],
        scratch_shapes=scratch,
        cost_estimate=pl.CostEstimate(
            flops=(blocks - 1) * flops, bytes_accessed=6 << 20, transcendentals=0
        ),
        compiler_params=pltpu.CompilerParams(vmem_limit_bytes=MOST_VMEM),
        name="later",
    )(frames, frames, taps, *weights)
    head = lambda n: pl.BlockSpec((TILE, n), lambda i: (i, 0))
    anywhere = pl.BlockSpec(memory_space=pl.ANY)
    flat = pl.BlockSpec((HEAD_DIM, HEAD_DIM), lambda i: (0, 0))
    before = 5 + len(weights)
    *longs, first_state, total = pl.pallas_call(
        first_kernel,
        grid=(PER_BLOCK,),
        in_specs=[
            head(width),
            pl.BlockSpec((EDGE, width), lambda i: (jnp.maximum(i * per - 1, 0), 0)),
            whole(edge),
            whole(taps),
        ]
        + [whole(w) for w in weights]
        + [whole(states)]
        + [anywhere] * 4,
        out_specs=[head(HEAD_DIM)] * 4 + [flat, flat],
        out_shape=long_shapes + [square, square],
        input_output_aliases={before + i: i for i in range(4)},
        scratch_shapes=scratch,
        compiler_params=pltpu.CompilerParams(vmem_limit_bytes=MOST_VMEM),
        name="first",
    )(frames, frames, edge, taps, *weights, states, *longs)
    return longs, first_state, states, total


def inner_kernel(q_ref, k_ref, v_ref, g_ref, gain_ref, intra_ref, gate_ref):
    queries = q_ref[...]
    keys = k_ref[...]
    values = v_ref[...]
    gates = g_ref[...]
    gate_ref[...] = gates / (1.0 + jnp.exp(-gates)) * gain_ref[...]
    half = BLOCK // 2
    row = lax.broadcasted_iota(jnp.int32, (half, half), 0)
    col = lax.broadcasted_iota(jnp.int32, (half, half), 1)
    causal = col <= row

    def scores_of(a, b):
        return lax.dot_general(a, b, (((1,), (1,)), ((), ())), preferred_element_type=F32)

    top, bottom = slice(0, half), slice(half, BLOCK)
    first = jnp.where(causal, scores_of(queries[top], keys[top]), 0.0).astype(BF16)
    intra_ref[top, :] = jnp.dot(first, values[top], preferred_element_type=F32)
    cross = scores_of(queries[bottom], keys[top]).astype(BF16)
    last = jnp.where(causal, scores_of(queries[bottom], keys[bottom]), 0.0).astype(BF16)
    both = jnp.concatenate([cross, last], axis=1)
    intra_ref[bottom, :] = jnp.dot(both, values, preferred_element_type=F32)


def inner(q, k, v, g, gain):
    rows = q.shape[0]
    tile = pl.BlockSpec((BLOCK, HEAD_DIM), lambda i: (i, 0))
    return pl.pallas_call(
        inner_kernel,
        grid=(rows // BLOCK,),
        in_specs=[tile] * 4 + [pl.BlockSpec(gain.shape, lambda i: (0, 0))],
        out_specs=[tile, tile],
        out_shape=[pltpu.HBM((rows, HEAD_DIM), F32)] * 2,
        cost_estimate=pl.CostEstimate(
            flops=2 * rows * BLOCK * 2 * HEAD_DIM, bytes_accessed=5 << 20, transcendentals=0
        ),
        compiler_params=pltpu.CompilerParams(vmem_limit_bytes=MOST_VMEM),
        name="inner",
    )(q, k, v, g, gain)


def spread_kernel(members, groups, place_ref, x_ref, o_ref):
    size = x_ref.shape[0]
    rows_per = size // members
    group = place_ref[0] // members
    row = lax.broadcasted_iota(jnp.int32, x_ref.shape, 0)

    def shifted(value, by):
        return jnp.where(row >= by, pltpu.roll(value, by, 0), 0.0)

    own = x_ref[...]
    before = shifted(own, rows_per)
    by = rows_per
    while by < size:
        before = before + shifted(before, by)
        by *= 2
    total = (before + own)[size - rows_per :]
    total = jnp.concatenate([total] * members, axis=0)
    for other in range(groups):
        scale = jnp.where(other > group, 1.0, 0.0)
        value = jnp.where(other == group, before, total * scale)
        o_ref[other * size : (other + 1) * size, :] = value.astype(BF16)


MEMBERS = 16


def near_exchange(own_total):
    devices = lax.axis_size("tm")
    groups = devices // MEMBERS
    near = [[g * MEMBERS + m for m in range(MEMBERS)] for g in range(groups)]
    parts = own_total.reshape(MEMBERS, HEAD_DIM // MEMBERS, HEAD_DIM)
    with jax.named_scope("near"):
        return lax.all_to_all(parts, "tm", 0, 0, axis_index_groups=near)


def spread_sums(theirs):
    groups = lax.axis_size("tm") // MEMBERS
    return pl.pallas_call(
        functools.partial(spread_kernel, MEMBERS, groups),
        in_specs=[pl.BlockSpec(memory_space=pltpu.SMEM), pl.BlockSpec(memory_space=pltpu.VMEM)],
        out_shape=jax.ShapeDtypeStruct((groups * HEAD_DIM, HEAD_DIM), BF16),
        compiler_params=pltpu.CompilerParams(vmem_limit_bytes=4 << 20),
        name="spread",
    )(lax.axis_index("tm").reshape(1), theirs.reshape(HEAD_DIM, HEAD_DIM))


def far_exchange(spread):
    devices = lax.axis_size("tm")
    with jax.named_scope("far"):
        back = lax.all_to_all(spread.reshape(devices, -1, HEAD_DIM), "tm", 0, 0)
    return back.reshape(-1, HEAD_DIM, HEAD_DIM)


def finish_kernel(q_ref, intra_ref, gate_ref, first_ref, later_ref, incoming_ref, o_ref, running):
    step = pl.program_id(0)

    @pl.when(step == 0)
    def _():
        running[...] = jnp.sum(incoming_ref[...].astype(F32), axis=0)

    carried = running[...].astype(BF16)
    running[...] += jnp.where(step == 0, first_ref[...], later_ref[0])
    attended = intra_ref[...] + jnp.dot(q_ref[...], carried, preferred_element_type=F32)
    mean_square = jnp.mean(attended * attended, axis=-1, keepdims=True)
    o_ref[...] = (attended * lax.rsqrt(mean_square + 1e-06) * gate_ref[...]).astype(BF16)


def finish(q, intra, gate, first_state, states, incoming):
    rows = q.shape[0]
    tile = pl.BlockSpec((BLOCK, HEAD_DIM), lambda i: (i, 0))
    whole = lambda a: pl.BlockSpec(a.shape, lambda i: (0,) * a.ndim)
    return pl.pallas_call(
        finish_kernel,
        grid=(rows // BLOCK,),
        in_specs=[
            tile,
            tile,
            tile,
            whole(first_state),
            pl.BlockSpec((1, HEAD_DIM, HEAD_DIM), lambda i: (jnp.maximum(i - 1, 0), 0, 0)),
            whole(incoming),
        ],
        out_specs=tile,
        out_shape=jax.ShapeDtypeStruct((rows, HEAD_DIM), BF16),
        scratch_shapes=[pltpu.VMEM((HEAD_DIM, HEAD_DIM), F32)],
        compiler_params=pltpu.CompilerParams(vmem_limit_bytes=MOST_VMEM),
        name="finish",
    )(q, intra, gate, first_state, states, incoming)


def early_kernel(own, left_top, left_bottom, right_top, right_bottom, w_own, w_left, w_right, acc):
    upper = pl.program_id(0) < pl.num_programs(0) // 2
    left = jnp.where(upper, left_top[...], left_bottom[...])
    right = jnp.where(upper, right_top[...], right_bottom[...])
    total = jnp.dot(own[...], w_own[...], preferred_element_type=F32)
    total += jnp.dot(left, w_left[...], preferred_element_type=F32)
    acc[...] = total + jnp.dot(right, w_right[...], preferred_element_type=F32)


def late_kernel(acc, far_top, far_bottom, w, keep, give):
    upper = pl.program_id(0) < pl.num_programs(0) // 2
    far = jnp.where(upper, far_top[...], far_bottom[...])
    total = acc[...] + jnp.dot(far, w[...], preferred_element_type=F32)
    keep[...] = total[:, :HEAD_DIM]
    give[...] = total[:, HEAD_DIM:].astype(BF16)


def project_early(own, lefts, rights, weights):
    rows = own.shape[0]
    steps = rows // BLOCK
    tile = lambda n: pl.BlockSpec((BLOCK, n), lambda i: (i, 0))
    upper = pl.BlockSpec((BLOCK, HEAD_DIM), lambda i: (jnp.minimum(i, steps // 2 - 1), 0))
    lower = pl.BlockSpec((BLOCK, HEAD_DIM), lambda i: (jnp.maximum(i - steps // 2, 0), 0))
    whole = pl.BlockSpec((HEAD_DIM, 2 * HEAD_DIM), lambda i: (0, 0))
    return pl.pallas_call(
        early_kernel,
        grid=(steps,),
        in_specs=[tile(HEAD_DIM), upper, lower, upper, lower] + [whole] * 3,
        out_specs=tile(2 * HEAD_DIM),
        out_shape=jax.ShapeDtypeStruct((rows, 2 * HEAD_DIM), F32),
        cost_estimate=pl.CostEstimate(
            flops=2 * rows * 6 * HEAD_DIM * HEAD_DIM, bytes_accessed=5 << 20, transcendentals=0
        ),
        compiler_params=pltpu.CompilerParams(vmem_limit_bytes=16 << 20),
        name="early",
    )(own, *lefts, *rights, *weights)


def project_late(acc, far_top, far_bottom, weights):
    rows = acc.shape[0]
    steps = rows // BLOCK
    tile = lambda n: pl.BlockSpec((BLOCK, n), lambda i: (i, 0))
    upper = pl.BlockSpec((BLOCK, HEAD_DIM), lambda i: (jnp.minimum(i, steps // 2 - 1), 0))
    lower = pl.BlockSpec((BLOCK, HEAD_DIM), lambda i: (jnp.maximum(i - steps // 2, 0), 0))
    whole = pl.BlockSpec((HEAD_DIM, 2 * HEAD_DIM), lambda i: (0, 0))
    return pl.pallas_call(
        late_kernel,
        grid=(steps,),
        in_specs=[tile(2 * HEAD_DIM), upper, lower, whole],
        out_specs=[tile(HEAD_DIM), tile(HEAD_DIM)],
        out_shape=[
            jax.ShapeDtypeStruct((rows, HEAD_DIM), F32),
            jax.ShapeDtypeStruct((rows, HEAD_DIM), BF16),
        ],
        compiler_params=pltpu.CompilerParams(vmem_limit_bytes=16 << 20),
        name="late",
    )(acc, far_top, far_bottom, weights)


def on_device(frames, conv_weight, w_query, w_key, w_value, w_gate, w_out, norm_gain):
    tok_rows, width = frames.shape
    times = lax.axis_size("tm")
    chips = lax.axis_size("head") // CORES
    head = lax.axis_index("head")
    chip, core = head // CORES, head % CORES

    def along(array, by):
        pairs = [
            (y * CORES + c, (y + by) % chips * CORES + c)
            for y in range(chips)
            for c in range(CORES)
        ]
        return lax.ppermute(array, "head", pairs)

    def swap(array):
        pairs = [(h, h ^ 1) for h in range(chips * CORES)]
        return lax.ppermute(array, "head", pairs)

    def columns_for(w_out, by):
        at = (chip + by) % chips
        mine = lax.dynamic_slice_in_dim(w_out, (at * CORES + core) * HEAD_DIM, HEAD_DIM, 1)
        other = lax.dynamic_slice_in_dim(w_out, (at * CORES + 1 - core) * HEAD_DIM, HEAD_DIM, 1)
        return jnp.concatenate([mine, other], axis=1)

    hbm = lambda a: pltpu.with_memory_space_constraint(a, pltpu.HBM)
    edge = lax.ppermute(
        frames[tok_rows - EDGE :], "tm", [(i, i + 1) for i in range(times - 1)]
    )
    weights = tuple(hbm(w) for w in (w_key, w_value, w_query, w_gate))
    longs, first_state, states, total = front(hbm(frames), edge, hbm(conv_weight), weights)
    q, keys, values, g = (hbm(a) for a in longs)
    theirs = near_exchange(total)
    intra, gate = inner(q, keys, values, g, hbm(norm_gain.reshape(1, HEAD_DIM)))
    theirs, intra, gate = lax.optimization_barrier((theirs, intra, gate))
    spread = spread_sums(theirs)
    incoming = far_exchange(spread)
    w_out, spread = lax.optimization_barrier((w_out, spread))
    w_far = columns_for(w_out, 2)
    to_right = jnp.concatenate([columns_for(w_out, 1), w_far[:, :HEAD_DIM]], axis=1)
    to_left = jnp.concatenate([columns_for(w_out, -1), w_far[:, HEAD_DIM:]], axis=1)
    w_left = along(to_right, 1)
    w_right = along(to_left, -1)
    incoming, w_left, w_right = lax.optimization_barrier((incoming, w_left, w_right))
    w_own = columns_for(w_out, 0)
    gated = finish(q, hbm(intra), hbm(gate), first_state, states, incoming)

    half = tok_rows // 2
    upper, lower = gated[:half], gated[half:]
    left_top = along(upper, 1)
    right_bottom = along(lower, -1)
    left_bottom = along(lower, 1)
    right_top = along(upper, -1)
    pair = 2 * HEAD_DIM
    far_top = along(jnp.concatenate([left_top, w_left[:, pair:]], axis=0), 1)
    far_bottom = along(jnp.concatenate([right_bottom, w_right[:, pair:]], axis=0), -1)
    acc = project_early(
        gated,
        (left_top, left_bottom),
        (right_top, right_bottom),
        (w_own, w_left[:, :pair], w_right[:, :pair]),
    )
    w_far = jnp.concatenate([far_top[half:], far_bottom[half:]], axis=1)
    keep, give = project_late(acc, far_top, far_bottom, w_far)
    return (keep + swap(give).astype(F32)).astype(BF16)


def solution(mesh):
    placed = (
        P("tm", None),
        P(),
        P(None, "head"),
        P(None, "head"),
        P(None, "head"),
        P(None, "head"),
        P("head", None),
        P("head"),
    )
    return jax.shard_map(
        on_device, mesh=mesh, in_specs=placed, out_specs=P("tm", "head"), check_vma=False
    )
```

```python
import functools

import jax
import jax.numpy as jnp
from jax import lax
from jax.experimental import pallas as pl
from jax.experimental.pallas import tpu as pltpu
from jax.sharding import PartitionSpec as P

HEAD_DIM = 128
CONV = 4
BLOCK = 512
CORES = 2
EDGE = 16
LANES = 128
TILE = 512
PER_BLOCK = BLOCK // TILE
MOST_VMEM = 44 << 20

F32 = jnp.float32
BF16 = jnp.bfloat16


def feature_map(inputs):
    return jnp.where(inputs > 0, inputs + 1.0, jnp.exp(jnp.minimum(inputs, 0.0)))


def projections(frames_ref, edge, taps_ref, joined, smooth, shifted, outs):
    width = frames_ref.shape[1]
    for lane in range(0, width, LANES):
        cols = slice(lane, lane + LANES)
        held = shifted.at[lane // LANES]
        taps = taps_ref[:, cols].astype(F32)
        own = frames_ref[:, cols].astype(F32)
        held[0:8, :] = edge[EDGE - 8 :, cols]
        held[8 : TILE + 8, :] = own
        mixed = taps[0:1] * held[5 : TILE + 5, :]
        mixed += taps[1:2] * held[6 : TILE + 6, :]
        mixed += taps[2:3] * held[7 : TILE + 7, :]
        mixed += taps[3:4] * own
        smooth[:, cols] = mixed.astype(BF16)
    product = jnp.dot(smooth[...], joined[...], preferred_element_type=F32)
    q_ref, k_ref, v_ref, g_ref = outs
    keys = feature_map(product[:, 0:HEAD_DIM]).astype(BF16)
    values = product[:, HEAD_DIM : 2 * HEAD_DIM].astype(BF16)
    q_ref[...] = feature_map(product[:, 2 * HEAD_DIM : 3 * HEAD_DIM]).astype(BF16)
    k_ref[...] = keys
    v_ref[...] = values
    g_ref[...] = product[:, 3 * HEAD_DIM :]
    return lax.dot_general(
        keys, values, (((0,), (0,)), ((), ())), preferred_element_type=F32
    )


def later_kernel(
    frames_ref, before_ref, taps_ref, wk, wv, wq, wg, q_ref, k_ref, v_ref, g_ref, state_ref,
    joined, smooth, shifted,
):
    step = pl.program_id(0)

    @pl.when(step == 0)
    def _():
        for place, ref in enumerate((wk, wv, wq, wg)):
            joined[:, place * HEAD_DIM : (place + 1) * HEAD_DIM] = ref[...]

    edge = before_ref[...].astype(F32)
    state = projections(
        frames_ref, edge, taps_ref, joined, smooth, shifted, (q_ref, k_ref, v_ref, g_ref)
    )

    @pl.when(step % PER_BLOCK == 0)
    def _():
        state_ref[0] = state

    @pl.when(step % PER_BLOCK != 0)
    def _():
        state_ref[0] += state


def first_kernel(
    frames_ref, before_ref, edge_ref, taps_ref, joined, states_ref, q_in, k_in, v_in, g_in,
    q_ref, k_ref, v_ref, g_ref, state_ref, total_ref, smooth, shifted,
):
    step = pl.program_id(0)
    edge = jnp.where(step == 0, edge_ref[...].astype(F32), before_ref[...].astype(F32))
    state = projections(
        frames_ref, edge, taps_ref, joined, smooth, shifted, (q_ref, k_ref, v_ref, g_ref)
    )

    @pl.when(step == 0)
    def _():
        state_ref[...] = state
        total_ref[...] = state + jnp.sum(states_ref[...], axis=0)

    @pl.when(step != 0)
    def _():
        state_ref[...] += state
        total_ref[...] += state


def front(frames, edge, taps, weights):
    rows, width = frames.shape
    blocks = rows // BLOCK
    per = TILE // EDGE
    whole = lambda a: pl.BlockSpec(a.shape, lambda i: (0,) * a.ndim)
    tile = lambda n: pl.BlockSpec((TILE, n), lambda i: (i + PER_BLOCK, 0))
    square = jax.ShapeDtypeStruct((HEAD_DIM, HEAD_DIM), F32)
    long_shapes = [pltpu.HBM((rows, HEAD_DIM), BF16)] * 3 + [pltpu.HBM((rows, HEAD_DIM), F32)]
    scratch = [
        pltpu.VMEM((TILE, width), BF16),
        pltpu.VMEM((width // LANES, TILE + 8, LANES), F32),
    ]
    anywhere = pl.BlockSpec(memory_space=pl.ANY)
    joined_shape = (width, len(weights) * HEAD_DIM)
    flops = 2 * BLOCK * width * 4 * HEAD_DIM
    *longs, states, joined = pl.pallas_call(
        later_kernel,
        grid=((blocks - 1) * PER_BLOCK,),
        in_specs=[
            tile(width),
            pl.BlockSpec((EDGE, width), lambda i: ((i + PER_BLOCK) * per - 1, 0)),
            whole(taps),
        ]
        + [whole(w) for w in weights],
        out_specs=[tile(HEAD_DIM)] * 4
        + [
            pl.BlockSpec((1, HEAD_DIM, HEAD_DIM), lambda i: (i // PER_BLOCK, 0, 0)),
            pl.BlockSpec(memory_space=pltpu.VMEM),
        ],
        out_shape=long_shapes
        + [
            jax.ShapeDtypeStruct((blocks - 1, HEAD_DIM, HEAD_DIM), F32),
            pltpu.VMEM(joined_shape, BF16),
        ],
        scratch_shapes=scratch,
        cost_estimate=pl.CostEstimate(
            flops=(blocks - 1) * flops, bytes_accessed=6 << 20, transcendentals=0
        ),
        compiler_params=pltpu.CompilerParams(vmem_limit_bytes=MOST_VMEM),
        name="later",
    )(frames, frames, taps, *weights)
    head = lambda n: pl.BlockSpec((TILE, n), lambda i: (i, 0))
    flat = pl.BlockSpec((HEAD_DIM, HEAD_DIM), lambda i: (0, 0))
    before = 6
    *longs, first_state, total = pl.pallas_call(
        first_kernel,
        grid=(PER_BLOCK,),
        in_specs=[
            head(width),
            pl.BlockSpec((EDGE, width), lambda i: (jnp.maximum(i * per - 1, 0), 0)),
            whole(edge),
            whole(taps),
        ]
        + [pl.BlockSpec(memory_space=pltpu.VMEM), whole(states)]
        + [anywhere] * 4,
        out_specs=[head(HEAD_DIM)] * 4 + [flat, flat],
        out_shape=long_shapes + [square, square],
        input_output_aliases={before + i: i for i in range(4)},
        scratch_shapes=scratch,
        compiler_params=pltpu.CompilerParams(vmem_limit_bytes=MOST_VMEM),
        name="first",
    )(frames, frames, edge, taps, joined, states, *longs)
    return longs, first_state, states, total


def inner_kernel(q_ref, k_ref, v_ref, g_ref, gain_ref, intra_ref, gate_ref, held_ref):
    queries = q_ref[...]
    held_ref[...] = queries
    keys = k_ref[...]
    values = v_ref[...]
    gates = g_ref[...]
    gate_ref[...] = gates / (1.0 + jnp.exp(-gates)) * gain_ref[...]
    half = BLOCK // 2
    row = lax.broadcasted_iota(jnp.int32, (half, half), 0)
    col = lax.broadcasted_iota(jnp.int32, (half, half), 1)
    causal = col <= row

    def scores_of(a, b):
        return lax.dot_general(a, b, (((1,), (1,)), ((), ())), preferred_element_type=F32)

    top, bottom = slice(0, half), slice(half, BLOCK)
    first = jnp.where(causal, scores_of(queries[top], keys[top]), 0.0).astype(BF16)
    intra_ref[top, :] = jnp.dot(first, values[top], preferred_element_type=F32)
    cross = scores_of(queries[bottom], keys[top]).astype(BF16)
    last = jnp.where(causal, scores_of(queries[bottom], keys[bottom]), 0.0).astype(BF16)
    both = jnp.concatenate([cross, last], axis=1)
    intra_ref[bottom, :] = jnp.dot(both, values, preferred_element_type=F32)


def inner(q, k, v, g, gain):
    rows = q.shape[0]
    tile = pl.BlockSpec((BLOCK, HEAD_DIM), lambda i: (i, 0))
    return pl.pallas_call(
        inner_kernel,
        grid=(rows // BLOCK,),
        in_specs=[tile] * 4 + [pl.BlockSpec(gain.shape, lambda i: (0, 0))],
        out_specs=[tile, tile, tile],
        out_shape=[jax.ShapeDtypeStruct((rows, HEAD_DIM), F32)] * 2
        + [jax.ShapeDtypeStruct((rows, HEAD_DIM), BF16)],
        cost_estimate=pl.CostEstimate(
            flops=2 * rows * BLOCK * 2 * HEAD_DIM, bytes_accessed=5 << 20, transcendentals=0
        ),
        compiler_params=pltpu.CompilerParams(vmem_limit_bytes=MOST_VMEM),
        name="inner",
    )(q, k, v, g, gain)


def spread_kernel(members, groups, x_ref, o_ref):
    size = x_ref.shape[0]
    rows_per = size // members
    group = lax.axis_index("tm") // members
    row = lax.broadcasted_iota(jnp.int32, x_ref.shape, 0)

    def shifted(value, by):
        return jnp.where(row >= by, pltpu.roll(value, by, 0), 0.0)

    own = x_ref[...]
    before = shifted(own, rows_per)
    by = rows_per
    while by < size:
        before = before + shifted(before, by)
        by *= 2
    total = (before + own)[size - rows_per :]
    total = jnp.concatenate([total] * members, axis=0)
    for other in range(groups):
        scale = jnp.where(other > group, 1.0, 0.0)
        value = jnp.where(other == group, before, total * scale)
        o_ref[other * size : (other + 1) * size, :] = value.astype(BF16)


MEMBERS = 16


def near_exchange(own_total):
    devices = lax.axis_size("tm")
    groups = devices // MEMBERS
    near = [[g * MEMBERS + m for m in range(MEMBERS)] for g in range(groups)]
    parts = own_total.reshape(MEMBERS, HEAD_DIM // MEMBERS, HEAD_DIM)
    with jax.named_scope("near"):
        return lax.all_to_all(parts, "tm", 0, 0, axis_index_groups=near)


def spread_sums(theirs):
    groups = lax.axis_size("tm") // MEMBERS
    return pl.pallas_call(
        functools.partial(spread_kernel, MEMBERS, groups),
        out_shape=jax.ShapeDtypeStruct((groups * HEAD_DIM, HEAD_DIM), BF16),
        compiler_params=pltpu.CompilerParams(vmem_limit_bytes=4 << 20),
        name="spread",
    )(theirs.reshape(HEAD_DIM, HEAD_DIM))


def far_exchange(spread):
    devices = lax.axis_size("tm")
    with jax.named_scope("far"):
        back = lax.all_to_all(spread.reshape(devices, -1, HEAD_DIM), "tm", 0, 0)
    return back.reshape(-1, HEAD_DIM, HEAD_DIM)


def finish_kernel(q_ref, intra_ref, gate_ref, first_ref, later_ref, incoming_ref, o_ref, running):
    step = pl.program_id(0)

    @pl.when(step == 0)
    def _():
        running[...] = jnp.sum(incoming_ref[...].astype(F32), axis=0)

    carried = running[...].astype(BF16)
    running[...] += jnp.where(step == 0, first_ref[...], later_ref[0])
    attended = intra_ref[...] + jnp.dot(q_ref[...], carried, preferred_element_type=F32)
    mean_square = jnp.mean(attended * attended, axis=-1, keepdims=True)
    o_ref[...] = (attended * lax.rsqrt(mean_square + 1e-06) * gate_ref[...]).astype(BF16)


def finish(q, intra, gate, first_state, states, incoming):
    rows = q.shape[0]
    tile = pl.BlockSpec((BLOCK, HEAD_DIM), lambda i: (i, 0))
    whole = lambda a: pl.BlockSpec(a.shape, lambda i: (0,) * a.ndim)
    return pl.pallas_call(
        finish_kernel,
        grid=(rows // BLOCK,),
        in_specs=[
            tile,
            tile,
            tile,
            whole(first_state),
            pl.BlockSpec((1, HEAD_DIM, HEAD_DIM), lambda i: (jnp.maximum(i - 1, 0), 0, 0)),
            whole(incoming),
        ],
        out_specs=tile,
        out_shape=jax.ShapeDtypeStruct((rows, HEAD_DIM), BF16),
        scratch_shapes=[pltpu.VMEM((HEAD_DIM, HEAD_DIM), F32)],
        compiler_params=pltpu.CompilerParams(vmem_limit_bytes=16 << 20),
        name="finish",
    )(q, intra, gate, first_state, states, incoming)


def early_kernel(own, left_top, left_bottom, right_top, right_bottom, w_own, w_left, w_right, acc):
    upper = pl.program_id(0) < pl.num_programs(0) // 2
    left = jnp.where(upper, left_top[...], left_bottom[...])
    right = jnp.where(upper, right_top[...], right_bottom[...])
    total = jnp.dot(own[...], w_own[...], preferred_element_type=F32)
    total += jnp.dot(left, w_left[...], preferred_element_type=F32)
    acc[...] = total + jnp.dot(right, w_right[...], preferred_element_type=F32)


def late_kernel(acc, far_top, far_bottom, w, keep, give):
    upper = pl.program_id(0) < pl.num_programs(0) // 2
    far = jnp.where(upper, far_top[...], far_bottom[...])
    total = acc[...] + jnp.dot(far, w[...], preferred_element_type=F32)
    keep[...] = total[:, :HEAD_DIM]
    give[...] = total[:, HEAD_DIM:].astype(BF16)


def project_early(own, lefts, rights, weights):
    rows = own.shape[0]
    steps = rows // BLOCK
    tile = lambda n: pl.BlockSpec((BLOCK, n), lambda i: (i, 0))
    upper = pl.BlockSpec((BLOCK, HEAD_DIM), lambda i: (jnp.minimum(i, steps // 2 - 1), 0))
    lower = pl.BlockSpec((BLOCK, HEAD_DIM), lambda i: (jnp.maximum(i - steps // 2, 0), 0))
    whole = pl.BlockSpec((HEAD_DIM, 2 * HEAD_DIM), lambda i: (0, 0))
    return pl.pallas_call(
        early_kernel,
        grid=(steps,),
        in_specs=[tile(HEAD_DIM), upper, lower, upper, lower] + [whole] * 3,
        out_specs=tile(2 * HEAD_DIM),
        out_shape=jax.ShapeDtypeStruct((rows, 2 * HEAD_DIM), F32),
        cost_estimate=pl.CostEstimate(
            flops=2 * rows * 6 * HEAD_DIM * HEAD_DIM, bytes_accessed=5 << 20, transcendentals=0
        ),
        compiler_params=pltpu.CompilerParams(vmem_limit_bytes=16 << 20),
        name="early",
    )(own, *lefts, *rights, *weights)


def project_late(acc, far_top, far_bottom, weights):
    rows = acc.shape[0]
    steps = rows // BLOCK
    tile = lambda n: pl.BlockSpec((BLOCK, n), lambda i: (i, 0))
    upper = pl.BlockSpec((BLOCK, HEAD_DIM), lambda i: (jnp.minimum(i, steps // 2 - 1), 0))
    lower = pl.BlockSpec((BLOCK, HEAD_DIM), lambda i: (jnp.maximum(i - steps // 2, 0), 0))
    whole = pl.BlockSpec((HEAD_DIM, 2 * HEAD_DIM), lambda i: (0, 0))
    return pl.pallas_call(
        late_kernel,
        grid=(steps,),
        in_specs=[tile(2 * HEAD_DIM), upper, lower, whole],
        out_specs=[tile(HEAD_DIM), tile(HEAD_DIM)],
        out_shape=[
            jax.ShapeDtypeStruct((rows, HEAD_DIM), F32),
            jax.ShapeDtypeStruct((rows, HEAD_DIM), BF16),
        ],
        compiler_params=pltpu.CompilerParams(vmem_limit_bytes=16 << 20),
        name="late",
    )(acc, far_top, far_bottom, weights)


def on_device(frames, conv_weight, w_query, w_key, w_value, w_gate, w_out, norm_gain):
    tok_rows, width = frames.shape
    times = lax.axis_size("tm")
    chips = lax.axis_size("head") // CORES
    head = lax.axis_index("head")
    chip, core = head // CORES, head % CORES

    def along(array, by):
        pairs = [
            (y * CORES + c, (y + by) % chips * CORES + c)
            for y in range(chips)
            for c in range(CORES)
        ]
        return lax.ppermute(array, "head", pairs)

    def swap(array):
        pairs = [(h, h ^ 1) for h in range(chips * CORES)]
        return lax.ppermute(array, "head", pairs)

    def columns_for(w_out, by):
        at = (chip + by) % chips
        mine = lax.dynamic_slice_in_dim(w_out, (at * CORES + core) * HEAD_DIM, HEAD_DIM, 1)
        other = lax.dynamic_slice_in_dim(w_out, (at * CORES + 1 - core) * HEAD_DIM, HEAD_DIM, 1)
        return jnp.concatenate([mine, other], axis=1)

    hbm = lambda a: pltpu.with_memory_space_constraint(a, pltpu.HBM)
    edge = lax.ppermute(
        frames[tok_rows - EDGE :], "tm", [(i, i + 1) for i in range(times - 1)]
    )
    weights = tuple(hbm(w) for w in (w_key, w_value, w_query, w_gate))
    longs, first_state, states, total = front(hbm(frames), edge, hbm(conv_weight), weights)
    q, keys, values, g = (hbm(a) for a in longs)
    theirs = near_exchange(total)
    intra, gate, q = inner(q, keys, values, g, hbm(norm_gain.reshape(1, HEAD_DIM)))
    theirs, intra, gate, q = lax.optimization_barrier((theirs, intra, gate, q))
    spread = spread_sums(theirs)
    incoming = far_exchange(spread)
    w_out, spread = lax.optimization_barrier((w_out, spread))
    w_far = columns_for(w_out, 2)
    to_right = jnp.concatenate([columns_for(w_out, 1), w_far[:, :HEAD_DIM]], axis=1)
    to_left = jnp.concatenate([columns_for(w_out, -1), w_far[:, HEAD_DIM:]], axis=1)
    w_left = along(to_right, 1)
    w_right = along(to_left, -1)
    incoming, w_left, w_right = lax.optimization_barrier((incoming, w_left, w_right))
    w_own = columns_for(w_out, 0)
    gated = finish(q, intra, gate, first_state, states, incoming)

    half = tok_rows // 2
    upper, lower = gated[:half], gated[half:]
    left_top = along(upper, 1)
    right_bottom = along(lower, -1)
    left_bottom = along(lower, 1)
    right_top = along(upper, -1)
    pair = 2 * HEAD_DIM
    far_top = along(jnp.concatenate([left_top, w_left[:, pair:]], axis=0), 1)
    far_bottom = along(jnp.concatenate([right_bottom, w_right[:, pair:]], axis=0), -1)
    acc = project_early(
        gated,
        (left_top, left_bottom),
        (right_top, right_bottom),
        (w_own, w_left[:, :pair], w_right[:, :pair]),
    )
    w_far = jnp.concatenate([far_top[half:], far_bottom[half:]], axis=1)
    keep, give = project_late(acc, far_top, far_bottom, w_far)
    return (keep + swap(give).astype(F32)).astype(BF16)


def solution(mesh):
    placed = (
        P("tm", None),
        P(),
        P(None, "head"),
        P(None, "head"),
        P(None, "head"),
        P(None, "head"),
        P("head", None),
        P("head"),
    )
    return jax.shard_map(
        on_device, mesh=mesh, in_specs=placed, out_specs=P("tm", "head"), check_vma=False
    )
```

```python
import functools

import jax
import jax.numpy as jnp
from jax import lax
from jax.experimental import pallas as pl
from jax.experimental.pallas import tpu as pltpu
from jax.sharding import PartitionSpec as P

HEAD_DIM = 128
CONV = 4
BLOCK = 512
CORES = 2
EDGE = 16
LANES = 128
TILE = BLOCK
PER_BLOCK = BLOCK // TILE
MOST_VMEM = 44 << 20

F32 = jnp.float32
BF16 = jnp.bfloat16


def feature_map(inputs):
    return jnp.where(inputs > 0, inputs + 1.0, jnp.exp(jnp.minimum(inputs, 0.0)))


def projections(frames_ref, edge, taps_ref, joined, smooth, shifted, outs):
    width = frames_ref.shape[1]
    for lane in range(0, width, LANES):
        cols = slice(lane, lane + LANES)
        held = shifted.at[lane // LANES]
        taps = taps_ref[:, cols].astype(F32)
        own = frames_ref[:, cols].astype(F32)
        held[0:8, :] = edge[EDGE - 8 :, cols]
        held[8 : TILE + 8, :] = own
        mixed = taps[0:1] * held[5 : TILE + 5, :]
        mixed += taps[1:2] * held[6 : TILE + 6, :]
        mixed += taps[2:3] * held[7 : TILE + 7, :]
        mixed += taps[3:4] * own
        smooth[:, cols] = mixed.astype(BF16)
    product = jnp.dot(smooth[...], joined[...], preferred_element_type=F32)
    q_ref, k_ref, v_ref, g_ref = outs
    keys = feature_map(product[:, 0:HEAD_DIM]).astype(BF16)
    values = product[:, HEAD_DIM : 2 * HEAD_DIM].astype(BF16)
    q_ref[...] = feature_map(product[:, 2 * HEAD_DIM : 3 * HEAD_DIM]).astype(BF16)
    k_ref[...] = keys
    v_ref[...] = values
    g_ref[...] = product[:, 3 * HEAD_DIM :]
    return lax.dot_general(
        keys, values, (((0,), (0,)), ((), ())), preferred_element_type=F32
    )


def later_kernel(
    frames_ref, before_ref, taps_ref, frames_all, wk, wv, wq, wg, q_ref, k_ref, v_ref, g_ref,
    state_ref, joined, head_ref, smooth, shifted, arrived,
):
    step = pl.program_id(0)
    head_copy = pltpu.make_async_copy(frames_all.at[0:TILE, :], head_ref, arrived)

    @pl.when(step == 0)
    def _():
        head_copy.start()
        for place, ref in enumerate((wk, wv, wq, wg)):
            joined[:, place * HEAD_DIM : (place + 1) * HEAD_DIM] = ref[...]

    edge = before_ref[...].astype(F32)
    state = projections(
        frames_ref, edge, taps_ref, joined, smooth, shifted, (q_ref, k_ref, v_ref, g_ref)
    )

    state_ref[0] = state

    @pl.when(step == pl.num_programs(0) - 1)
    def _():
        head_copy.wait()


def first_kernel(
    head_ref, edge_ref, taps_ref, joined, states_ref, q_in, k_in, v_in, g_in,
    q_ref, k_ref, v_ref, g_ref, state_ref, total_ref, smooth, shifted,
):
    edge = edge_ref[...].astype(F32)
    outs = (q_ref, k_ref, v_ref, g_ref)
    state = projections(head_ref, edge, taps_ref, joined, smooth, shifted, outs)
    state_ref[...] = state
    total_ref[...] = state + jnp.sum(states_ref[...], axis=0)


def front(frames, edge, taps, weights):
    rows, width = frames.shape
    blocks = rows // BLOCK
    per = TILE // EDGE
    whole = lambda a: pl.BlockSpec(a.shape, lambda i: (0,) * a.ndim)
    tile = lambda n: pl.BlockSpec((TILE, n), lambda i: (i + PER_BLOCK, 0))
    square = pltpu.VMEM((HEAD_DIM, HEAD_DIM), F32)
    long_shapes = [pltpu.HBM((rows, HEAD_DIM), BF16)] * 3 + [pltpu.HBM((rows, HEAD_DIM), F32)]
    scratch = [
        pltpu.VMEM((TILE, width), BF16),
        pltpu.VMEM((width // LANES, TILE + 8, LANES), F32),
    ]
    anywhere = pl.BlockSpec(memory_space=pl.ANY)
    joined_shape = (width, len(weights) * HEAD_DIM)
    flops = 2 * BLOCK * width * 4 * HEAD_DIM
    *longs, states, joined, held = pl.pallas_call(
        later_kernel,
        grid=((blocks - 1) * PER_BLOCK,),
        in_specs=[
            tile(width),
            pl.BlockSpec((EDGE, width), lambda i: ((i + PER_BLOCK) * per - 1, 0)),
            whole(taps),
            anywhere,
        ]
        + [whole(w) for w in weights],
        out_specs=[tile(HEAD_DIM)] * 4
        + [
            pl.BlockSpec((1, HEAD_DIM, HEAD_DIM), lambda i: (i // PER_BLOCK, 0, 0)),
            pl.BlockSpec(memory_space=pltpu.VMEM),
            pl.BlockSpec(memory_space=pltpu.VMEM),
        ],
        out_shape=long_shapes
        + [
            jax.ShapeDtypeStruct((blocks - 1, HEAD_DIM, HEAD_DIM), F32),
            pltpu.VMEM(joined_shape, BF16),
            pltpu.VMEM((TILE, width), BF16),
        ],
        scratch_shapes=scratch + [pltpu.SemaphoreType.DMA(())],
        cost_estimate=pl.CostEstimate(
            flops=(blocks - 1) * flops, bytes_accessed=6 << 20, transcendentals=0
        ),
        compiler_params=pltpu.CompilerParams(vmem_limit_bytes=MOST_VMEM),
        name="later",
    )(frames, frames, taps, frames, *weights)
    head = lambda n: pl.BlockSpec((TILE, n), lambda i: (i, 0))
    flat = pl.BlockSpec((HEAD_DIM, HEAD_DIM), lambda i: (0, 0))
    before = 5
    *longs, first_state, total = pl.pallas_call(
        first_kernel,
        grid=(PER_BLOCK,),
        in_specs=[
            pl.BlockSpec(memory_space=pltpu.VMEM),
            whole(edge),
            whole(taps),
        ]
        + [pl.BlockSpec(memory_space=pltpu.VMEM), whole(states)]
        + [anywhere] * 4,
        out_specs=[head(HEAD_DIM)] * 4 + [flat, flat],
        out_shape=long_shapes + [square, square],
        input_output_aliases={before + i: i for i in range(4)},
        scratch_shapes=scratch,
        compiler_params=pltpu.CompilerParams(vmem_limit_bytes=MOST_VMEM),
        name="first",
    )(held, edge, taps, joined, states, *longs)
    return longs, first_state, states, total


def inner_kernel(q_ref, k_ref, v_ref, g_ref, gain_ref, intra_ref, gate_ref, held_ref):
    queries = q_ref[...]
    held_ref[...] = queries
    keys = k_ref[...]
    values = v_ref[...]
    gates = g_ref[...]
    gate_ref[...] = gates / (1.0 + jnp.exp(-gates)) * gain_ref[...]
    half = BLOCK // 2
    row = lax.broadcasted_iota(jnp.int32, (half, half), 0)
    col = lax.broadcasted_iota(jnp.int32, (half, half), 1)
    causal = col <= row

    def scores_of(a, b):
        return lax.dot_general(a, b, (((1,), (1,)), ((), ())), preferred_element_type=F32)

    top, bottom = slice(0, half), slice(half, BLOCK)
    first = jnp.where(causal, scores_of(queries[top], keys[top]), 0.0).astype(BF16)
    intra_ref[top, :] = jnp.dot(first, values[top], preferred_element_type=F32)
    cross = scores_of(queries[bottom], keys[top]).astype(BF16)
    last = jnp.where(causal, scores_of(queries[bottom], keys[bottom]), 0.0).astype(BF16)
    both = jnp.concatenate([cross, last], axis=1)
    intra_ref[bottom, :] = jnp.dot(both, values, preferred_element_type=F32)


def inner(q, k, v, g, gain):
    rows = q.shape[0]
    tile = pl.BlockSpec((BLOCK, HEAD_DIM), lambda i: (i, 0))
    return pl.pallas_call(
        inner_kernel,
        grid=(rows // BLOCK,),
        in_specs=[tile] * 4 + [pl.BlockSpec(gain.shape, lambda i: (0, 0))],
        out_specs=[tile, tile, tile],
        out_shape=[jax.ShapeDtypeStruct((rows, HEAD_DIM), F32)] * 2
        + [jax.ShapeDtypeStruct((rows, HEAD_DIM), BF16)],
        cost_estimate=pl.CostEstimate(
            flops=2 * rows * BLOCK * 2 * HEAD_DIM, bytes_accessed=5 << 20, transcendentals=0
        ),
        compiler_params=pltpu.CompilerParams(vmem_limit_bytes=MOST_VMEM),
        name="inner",
    )(q, k, v, g, gain)


def spread_kernel(members, groups, x_ref, o_ref):
    size = x_ref.shape[0]
    rows_per = size // members
    group = lax.axis_index("tm") // members
    row = lax.broadcasted_iota(jnp.int32, x_ref.shape, 0)

    def shifted(value, by):
        return jnp.where(row >= by, pltpu.roll(value, by, 0), 0.0)

    own = x_ref[...]
    before = shifted(own, rows_per)
    by = rows_per
    while by < size:
        before = before + shifted(before, by)
        by *= 2
    total = (before + own)[size - rows_per :]
    total = jnp.concatenate([total] * members, axis=0)
    for other in range(groups):
        scale = jnp.where(other > group, 1.0, 0.0)
        value = jnp.where(other == group, before, total * scale)
        o_ref[other * size : (other + 1) * size, :] = value.astype(BF16)


MEMBERS = 16


def near_exchange(own_total):
    devices = lax.axis_size("tm")
    groups = devices // MEMBERS
    near = [[g * MEMBERS + m for m in range(MEMBERS)] for g in range(groups)]
    parts = own_total.reshape(MEMBERS, HEAD_DIM // MEMBERS, HEAD_DIM)
    with jax.named_scope("near"):
        return lax.all_to_all(parts, "tm", 0, 0, axis_index_groups=near)


def spread_sums(theirs):
    groups = lax.axis_size("tm") // MEMBERS
    return pl.pallas_call(
        functools.partial(spread_kernel, MEMBERS, groups),
        out_shape=pltpu.VMEM((groups * HEAD_DIM, HEAD_DIM), BF16),
        compiler_params=pltpu.CompilerParams(vmem_limit_bytes=4 << 20),
        name="spread",
    )(theirs.reshape(HEAD_DIM, HEAD_DIM))


def far_exchange(spread):
    devices = lax.axis_size("tm")
    with jax.named_scope("far"):
        back = lax.all_to_all(spread.reshape(devices, -1, HEAD_DIM), "tm", 0, 0)
    return back.reshape(-1, HEAD_DIM, HEAD_DIM)


def finish_kernel(q_ref, intra_ref, gate_ref, first_ref, later_ref, incoming_ref, o_ref, running):
    step = pl.program_id(0)

    @pl.when(step == 0)
    def _():
        running[...] = jnp.sum(incoming_ref[...].astype(F32), axis=0)

    carried = running[...].astype(BF16)
    running[...] += jnp.where(step == 0, first_ref[...], later_ref[0])
    attended = intra_ref[...] + jnp.dot(q_ref[...], carried, preferred_element_type=F32)
    mean_square = jnp.mean(attended * attended, axis=-1, keepdims=True)
    o_ref[...] = (attended * lax.rsqrt(mean_square + 1e-06) * gate_ref[...]).astype(BF16)


def finish(q, intra, gate, first_state, states, incoming):
    rows = q.shape[0]
    tile = pl.BlockSpec((BLOCK, HEAD_DIM), lambda i: (i, 0))
    whole = lambda a: pl.BlockSpec(a.shape, lambda i: (0,) * a.ndim)
    return pl.pallas_call(
        finish_kernel,
        grid=(rows // BLOCK,),
        in_specs=[
            tile,
            tile,
            tile,
            whole(first_state),
            pl.BlockSpec((1, HEAD_DIM, HEAD_DIM), lambda i: (jnp.maximum(i - 1, 0), 0, 0)),
            whole(incoming),
        ],
        out_specs=tile,
        out_shape=jax.ShapeDtypeStruct((rows, HEAD_DIM), BF16),
        scratch_shapes=[pltpu.VMEM((HEAD_DIM, HEAD_DIM), F32)],
        compiler_params=pltpu.CompilerParams(vmem_limit_bytes=16 << 20),
        name="finish",
    )(q, intra, gate, first_state, states, incoming)


def early_kernel(own, left_top, left_bottom, right_top, right_bottom, w_own, w_left, w_right, acc):
    upper = pl.program_id(0) < pl.num_programs(0) // 2
    left = jnp.where(upper, left_top[...], left_bottom[...])
    right = jnp.where(upper, right_top[...], right_bottom[...])
    total = jnp.dot(own[...], w_own[...], preferred_element_type=F32)
    total += jnp.dot(left, w_left[...], preferred_element_type=F32)
    acc[...] = total + jnp.dot(right, w_right[...], preferred_element_type=F32)


def late_kernel(acc, far_top, far_bottom, w, keep, give):
    upper = pl.program_id(0) < pl.num_programs(0) // 2
    far = jnp.where(upper, far_top[...], far_bottom[...])
    total = acc[...] + jnp.dot(far, w[...], preferred_element_type=F32)
    keep[...] = total[:, :HEAD_DIM]
    give[...] = total[:, HEAD_DIM:].astype(BF16)


def project_early(own, lefts, rights, weights):
    rows = own.shape[0]
    steps = rows // BLOCK
    tile = lambda n: pl.BlockSpec((BLOCK, n), lambda i: (i, 0))
    upper = pl.BlockSpec((BLOCK, HEAD_DIM), lambda i: (jnp.minimum(i, steps // 2 - 1), 0))
    lower = pl.BlockSpec((BLOCK, HEAD_DIM), lambda i: (jnp.maximum(i - steps // 2, 0), 0))
    whole = pl.BlockSpec((HEAD_DIM, 2 * HEAD_DIM), lambda i: (0, 0))
    return pl.pallas_call(
        early_kernel,
        grid=(steps,),
        in_specs=[tile(HEAD_DIM), upper, lower, upper, lower] + [whole] * 3,
        out_specs=tile(2 * HEAD_DIM),
        out_shape=jax.ShapeDtypeStruct((rows, 2 * HEAD_DIM), F32),
        cost_estimate=pl.CostEstimate(
            flops=2 * rows * 6 * HEAD_DIM * HEAD_DIM, bytes_accessed=5 << 20, transcendentals=0
        ),
        compiler_params=pltpu.CompilerParams(vmem_limit_bytes=16 << 20),
        name="early",
    )(own, *lefts, *rights, *weights)


def project_late(acc, far_top, far_bottom, weights):
    rows = acc.shape[0]
    steps = rows // BLOCK
    tile = lambda n: pl.BlockSpec((BLOCK, n), lambda i: (i, 0))
    upper = pl.BlockSpec((BLOCK, HEAD_DIM), lambda i: (jnp.minimum(i, steps // 2 - 1), 0))
    lower = pl.BlockSpec((BLOCK, HEAD_DIM), lambda i: (jnp.maximum(i - steps // 2, 0), 0))
    whole = pl.BlockSpec((HEAD_DIM, 2 * HEAD_DIM), lambda i: (0, 0))
    return pl.pallas_call(
        late_kernel,
        grid=(steps,),
        in_specs=[tile(2 * HEAD_DIM), upper, lower, whole],
        out_specs=[tile(HEAD_DIM), tile(HEAD_DIM)],
        out_shape=[
            jax.ShapeDtypeStruct((rows, HEAD_DIM), F32),
            jax.ShapeDtypeStruct((rows, HEAD_DIM), BF16),
        ],
        compiler_params=pltpu.CompilerParams(vmem_limit_bytes=16 << 20),
        name="late",
    )(acc, far_top, far_bottom, weights)


def on_device(frames, conv_weight, w_query, w_key, w_value, w_gate, w_out, norm_gain):
    tok_rows, width = frames.shape
    times = lax.axis_size("tm")
    chips = lax.axis_size("head") // CORES
    head = lax.axis_index("head")
    chip, core = head // CORES, head % CORES

    def along(array, by):
        pairs = [
            (y * CORES + c, (y + by) % chips * CORES + c)
            for y in range(chips)
            for c in range(CORES)
        ]
        return lax.ppermute(array, "head", pairs)

    def swap(array):
        pairs = [(h, h ^ 1) for h in range(chips * CORES)]
        return lax.ppermute(array, "head", pairs)

    def columns_for(w_out, by):
        at = (chip + by) % chips
        mine = lax.dynamic_slice_in_dim(w_out, (at * CORES + core) * HEAD_DIM, HEAD_DIM, 1)
        other = lax.dynamic_slice_in_dim(w_out, (at * CORES + 1 - core) * HEAD_DIM, HEAD_DIM, 1)
        return jnp.concatenate([mine, other], axis=1)

    hbm = lambda a: pltpu.with_memory_space_constraint(a, pltpu.HBM)
    edge = lax.ppermute(
        frames[tok_rows - EDGE :], "tm", [(i, i + 1) for i in range(times - 1)]
    )
    weights = tuple(hbm(w) for w in (w_key, w_value, w_query, w_gate))
    longs, first_state, states, total = front(hbm(frames), edge, hbm(conv_weight), weights)
    q, keys, values, g = (hbm(a) for a in longs)
    theirs = near_exchange(total)
    intra, gate, q = inner(q, keys, values, g, hbm(norm_gain.reshape(1, HEAD_DIM)))
    theirs, intra, gate, q = lax.optimization_barrier((theirs, intra, gate, q))
    spread = spread_sums(theirs)
    incoming = far_exchange(spread)
    w_out, spread = lax.optimization_barrier((w_out, spread))
    w_far = columns_for(w_out, 2)
    to_right = jnp.concatenate([columns_for(w_out, 1), w_far[:, :HEAD_DIM]], axis=1)
    to_left = jnp.concatenate([columns_for(w_out, -1), w_far[:, HEAD_DIM:]], axis=1)
    w_left = along(to_right, 1)
    w_right = along(to_left, -1)
    incoming, w_left, w_right = lax.optimization_barrier((incoming, w_left, w_right))
    w_own = columns_for(w_out, 0)
    gated = finish(q, intra, gate, first_state, states, incoming)

    half = tok_rows // 2
    upper, lower = gated[:half], gated[half:]
    left_top = along(upper, 1)
    right_bottom = along(lower, -1)
    left_bottom = along(lower, 1)
    right_top = along(upper, -1)
    pair = 2 * HEAD_DIM
    far_top = along(jnp.concatenate([left_top, w_left[:, pair:]], axis=0), 1)
    far_bottom = along(jnp.concatenate([right_bottom, w_right[:, pair:]], axis=0), -1)
    acc = project_early(
        gated,
        (left_top, left_bottom),
        (right_top, right_bottom),
        (w_own, w_left[:, :pair], w_right[:, :pair]),
    )
    w_far = jnp.concatenate([far_top[half:], far_bottom[half:]], axis=1)
    keep, give = project_late(acc, far_top, far_bottom, w_far)
    return (keep + swap(give).astype(F32)).astype(BF16)


def solution(mesh):
    placed = (
        P("tm", None),
        P(),
        P(None, "head"),
        P(None, "head"),
        P(None, "head"),
        P(None, "head"),
        P("head", None),
        P("head"),
    )
    return jax.shard_map(
        on_device, mesh=mesh, in_specs=placed, out_specs=P("tm", "head"), check_vma=False
    )
```
